256 devices in a mesh: gx: 8 (over z_lo, x), gy: 32 (over y, z_hi, core).
Axes of the slice: x: 4, y: 4, z: 8 (z_hi: 4, z_lo: 2; z = z_hi * 2 + z_lo), core: 2. Of those that a mesh axis runs over, the one named last changes fastest.
Arguments:
- offsets: float32 [3, 16, 64, 2, 128], P(None, 'gx', 'gy'), may hold values from 0 to 1
- velocity: float32 [3, 16, 64, 2, 128], P(None, 'gx', 'gy'), may hold values from -6 to 6
- mass: float32 [16, 64, 2, 128], P('gx', 'gy'), may hold values from 0.00390625 to 0.03125
- energy: float32 [16, 64, 2, 128], P('gx', 'gy'), may hold values from 0.3 to 3
- counts: int32 [16, 64, 2], P('gx', 'gy'), may hold values from 1 to 128
Outputs:
- density: float32 [16, 64, 2, 128], P('gx', 'gy')
- acceleration: float32 [3, 16, 64, 2, 128], P(None, 'gx', 'gy')
- heating: float32 [16, 64, 2, 128], P('gx', 'gy')
The draws below stay inside these ranges and needn't reach their ends.
Inputs may be any that keep to these rules, and one draw needn't show every extreme that they name: Slots of a cell from counts on hold no particle.
All inputs are finite; a program needn't handle non-finite values.
Results may differ from the reference program's by a relative error of at most 0.0003.
Values sent between devices are 32-bit elements; how exact they have to be, the bound alone decides.
No kernel may reach another device: no remote copies, remote signals or barrier semaphores. Data moves between devices by JAX's collectives and lax.ppermute only.
A program may use at most 64 MiB of HBM per device.

```python
import math
import jax
import jax.numpy as jnp
from jax import lax

P_SIZE = 128
CZ = 2
NX = 16
NY = 64


def set_ends(values, own_key, smallest, top_value):
    spot = [jax.random.randint(jax.random.fold_in(own_key, axis), (), 0, length) for axis, length in enumerate(values.shape)]
    widest = values.shape.index(max(values.shape))
    next_to = spot[:widest] + [(spot[widest] + 1) % values.shape[widest]] + spot[widest + 1:]
    return values.at[tuple(spot)].set(smallest).at[tuple(next_to)].set(top_value)


def steps_of(stream_key, shape, shards, low, top_value):
    factor_of = 1.0
    for dim, shards_of in shards:
        draws = jax.random.uniform(jax.random.fold_in(jax.random.fold_in(stream_key, 6), dim), (shards_of,), jnp.float32, low / len(shards), top_value / len(shards))
        factor_of = factor_of * jnp.repeat(jnp.exp(draws), shape[dim] // shards_of).reshape((-1,) + (1,) * (len(shape) - 1 - dim))
    return factor_of


def normal_values(own_key, extent, deviation, bound, pieces=(), kind=jnp.bfloat16):
    entries = jax.random.normal(own_key, extent, jnp.float32) * deviation
    if len(pieces) > 0:
        entries = steps_of(own_key, extent, pieces, -0.22, 0.18) * entries
    return jnp.clip(entries, min=-bound, max=bound).astype(kind)


def setup_inputs(seed: int = 0) -> dict:
    seeds = jax.random.split(jax.random.key(seed), 6)
    return {
        "offsets": jnp.clip(1.0 * jax.random.uniform(seeds[0], (3, NX, NY, CZ, P_SIZE), jnp.float32) ** steps_of(seeds[0], (3, NX, NY, CZ, P_SIZE), ((1, 8), (2, 32)), -0.2, 0.2), 0.0, 1.0),
        "velocity": normal_values(seeds[1], (3, NX, NY, CZ, P_SIZE), 1.0, 6.0, ((1, 8), (2, 32)), jnp.float32),
        "mass": jnp.clip(jnp.exp(math.log(0.03125) - 2.0794415 * jax.random.uniform(seeds[2], (NX, NY, CZ, P_SIZE), jnp.float32) ** steps_of(seeds[2], (NX, NY, CZ, P_SIZE), ((0, 8), (1, 32)), -0.2, 0.2)), 0.00390625, 0.03125),
        "energy": jnp.clip(jnp.exp(math.log(3.0) - 2.3025851 * jax.random.uniform(seeds[3], (NX, NY, CZ, P_SIZE), jnp.float32) ** steps_of(seeds[3], (NX, NY, CZ, P_SIZE), ((0, 8), (1, 32)), -0.2, 0.2)), 0.3, 3.0),
        "counts": set_ends(jax.random.randint(seeds[4], (NX, NY, CZ), 1, P_SIZE + 1), jax.random.fold_in(seeds[4], 1), 1, P_SIZE).astype(jnp.int32),
    }


SMOOTHING = 0.5
NORMALISE = 1.0 / (math.pi * 0.125)
ADIABATIC = 5.0 / 3.0
VISC_ALPHA = 1.0
VISC_BETA = 2.0
SOFTENING = 0.01

def offsets_list():
    result = []
    for shift_x in (-1, 0, 1):
        for shift_y in (-1, 0, 1):
            for shift_z in (-1, 0, 1):
                result.append((shift_x, shift_y, shift_z))
    return result

def density_terms(own_cell, near_cell, delta):
    step = jnp.asarray(delta, jnp.float32).reshape(3, 1, 1, 1)
    separation = own_cell[0:3, :, :, None] - near_cell[0:3, :, None, :] - step
    scaled = jnp.sqrt(lax.optimization_barrier(jnp.sum(separation * separation, axis=0))) / SMOOTHING
    outer = jnp.maximum(2.0 - scaled, 0.0)
    inner = jnp.maximum(1.0 - scaled, 0.0)
    kernel = NORMALISE * (0.25 * outer * outer * outer - inner * inner * inner)
    return lax.optimization_barrier(jnp.sum(kernel * near_cell[6][:, None, :], axis=-1))

def force_terms(own_cell, near_cell, delta):
    step = jnp.asarray(delta, jnp.float32).reshape(3, 1, 1, 1)
    separation = own_cell[0:3, :, :, None] - near_cell[0:3, :, None, :] - step
    relative = own_cell[3:6, :, :, None] - near_cell[3:6, :, None, :]
    distance_sq = lax.optimization_barrier(jnp.sum(separation * separation, axis=0))
    scaled = jnp.sqrt(distance_sq) / SMOOTHING
    safe_scaled = jnp.where(scaled < 1.0, 1.0, scaled)
    outer = jnp.maximum(2.0 - scaled, 0.0)
    slope = jnp.where(scaled < 1.0, -3.0 + 2.25 * scaled, -0.75 * outer * outer / safe_scaled)
    weight = near_cell[6][:, None, :] * (NORMALISE / (SMOOTHING * SMOOTHING)) * slope
    approach = lax.optimization_barrier(jnp.sum(relative * separation, axis=0))
    closing = SMOOTHING * jnp.minimum(approach, 0.0) / (distance_sq + SOFTENING * SMOOTHING * SMOOTHING)
    sound = 0.5 * (own_cell[8][:, :, None] + near_cell[8][:, None, :])
    mean_rho = 0.5 * (own_cell[9][:, :, None] + near_cell[9][:, None, :])
    viscous = (-VISC_ALPHA * sound * closing + VISC_BETA * closing * closing) / mean_rho
    pushing = weight * (own_cell[7][:, :, None] + near_cell[7][:, None, :] + viscous)
    accel = -lax.optimization_barrier(jnp.sum(pushing[None] * separation, axis=-1))
    heat = lax.optimization_barrier(jnp.sum(weight * (own_cell[7][:, :, None] + 0.5 * viscous) * approach, axis=-1))
    return jnp.concatenate([accel, heat[None]], axis=0)

def block_apply(extended, count_x, count_y, terms, rows_out):
    layers = extended.shape[3] - 2
    slots = extended.shape[4]

    def column(position):
        first = position // count_y
        second = position % count_y
        zero = jnp.zeros((), jnp.int32)
        neighbours = lax.dynamic_slice(extended, (zero, first, second, zero, zero), (extended.shape[0], 3, 3, layers + 2, slots))
        own_cell = neighbours[:, 1, 1, 1:layers + 1]
        total = jnp.zeros((rows_out, layers, slots), jnp.float32)
        for delta in offsets_list():
            near_cell = neighbours[:, 1 + delta[0], 1 + delta[1], 1 + delta[2]:1 + delta[2] + layers]
            total = total + terms(own_cell, near_cell, delta).reshape(rows_out, layers, slots)
        return total
    columns = lax.map(column, jnp.arange(count_x * count_y, dtype=jnp.int32))
    columns = columns.reshape(count_x, count_y, rows_out, layers, slots)
    return jnp.moveaxis(columns, 2, 0)

def force_inputs(particles, density_safe):
    energy_part = particles[7]
    pressure_term = (ADIABATIC - 1.0) * energy_part / density_safe
    sound = jnp.sqrt(ADIABATIC * (ADIABATIC - 1.0) * energy_part)
    return jnp.concatenate([particles[0:7], pressure_term[None], sound[None], density_safe[None]], axis=0)

def reference(offsets, velocity, mass, energy, counts):
    slots = mass.shape[-1]
    occupied = (jnp.arange(slots, dtype=jnp.int32)[None, None, None, :] < counts[..., None]).astype(jnp.float32)
    particles = jnp.concatenate([offsets, velocity, (mass * occupied)[None], energy[None]], axis=0)
    extended = jnp.pad(particles, ((0, 0), (1, 1), (1, 1), (0, 0), (0, 0)), mode='wrap')
    extended = jnp.pad(extended, ((0, 0), (0, 0), (0, 0), (1, 1), (0, 0)))
    count_x = mass.shape[0]
    count_y = mass.shape[1]
    density = block_apply(extended, count_x, count_y, density_terms, 1)[0]
    density_safe = jnp.where(particles[6] > 0.0, density, 1.0)
    density_wide = jnp.pad(density_safe, ((1, 1), (1, 1), (0, 0), (0, 0)), mode='wrap')
    density_wide = jnp.pad(density_wide, ((0, 0), (0, 0), (1, 1), (0, 0)), constant_values=1.0)
    forces = block_apply(force_inputs(extended, density_wide), count_x, count_y, force_terms, 4)
    return (density * occupied, forces[0:3] * occupied[None], forces[3] * occupied)
```

```python
import functools
import math

import jax
import jax.numpy as jnp
from jax import lax
from jax.experimental import pallas as pl
from jax.experimental.pallas import tpu as pltpu
from jax.sharding import PartitionSpec as P

F = jnp.float32
SIGMA = 8.0 / math.pi
DENS_UNROLL = 8
FORCE_UNROLL = 4
CHUNK = 32
GROUPS = 16 * 2 * 16 + 4 * 8 + 2 * CHUNK
TARGETS = [(a, b) for a in (0, 1) for b in (0, 1)]


def cell_id(r, s, z):
    return (r * 4 + s) * 2 + z


def place(e_ref, c, tile, r, s, z):
    row = lax.broadcasted_iota(jnp.int32, (8, 128), 0)
    base = jnp.where(row == 0, F(r - 2), jnp.where(row == 1, F(s - 2), F(z - 1)))
    e_ref[c] = jnp.where(row < 3, 2.0 * (tile + base), tile)


def cell_counts(e_ref):
    masses = e_ref[:, 6, :]
    filled = jnp.sum(jnp.where(masses > 0.0, 1.0, 0.0), axis=1, keepdims=True)
    groups = lax.shift_right_logical(filled.astype(jnp.int32) + 7, 3)
    return [groups[c, 0] for c in range(32)]


def pad_tile(values):
    lane = lax.broadcasted_iota(jnp.int32, (8, len(values)), 1)
    tile = jnp.zeros((8, len(values)), F)
    for k, value in enumerate(values):
        if value:
            tile = jnp.where(lane == k, F(value), tile)
    return tile


def pack(groups, tile_of, t_ref, unroll, pad):
    width = pad.shape[1]
    starts = []
    base = jnp.int32(0)
    for r in range(4):
        row = []
        for s in range(4):
            row.append(base)
            for z in range(2):
                c = cell_id(r, s, z)
                turned = tile_of(c).T
                for g in range(16):
                    t_ref[base + g, :, 0:width] = turned[8 * g : 8 * g + 8, :]
                base = base + groups[c]
        row.append(base)
        for g in range(unroll - 1):
            t_ref[base + g, :, 0:width] = pad
        base = base + (unroll - 1)
        starts.append(row)
    return starts, base


def spread(t_ref, j_ref, total, attrs):
    def body(i, carry):
        for n, k in enumerate(attrs):
            for g in range(CHUNK):
                at = i * CHUNK + g
                j_ref[n, at] = jnp.broadcast_to(t_ref[at, :, k : k + 1], (8, 128))
        return carry

    lax.fori_loop(0, (total + CHUNK - 1) // CHUNK, body, 0)


def density_kernel(own_ref, up_ref, right_ref, rho_ref, e_ref, t_ref, j_ref):
    for r in range(4):
        for s in range(4):
            for z in range(2):
                if r >= 2:
                    tile = right_ref[r - 2, s, z]
                elif s >= 2:
                    tile = up_ref[r, s - 2, z]
                else:
                    tile = own_ref[r, s, z]
                place(e_ref, cell_id(r, s, z), tile, r, s, z)
    groups = cell_counts(e_ref)
    starts, total = pack(
        groups, lambda c: e_ref[c], t_ref, DENS_UNROLL, pad_tile((1e3, 1e3, 1e3, 0, 0, 0, 0, 0))
    )
    spread(t_ref, j_ref, total, (0, 1, 2, 6))
    for n, (a, b) in enumerate(TARGETS):
        own = [cell_id(1 + a, 1 + b, z) for z in (0, 1)]
        mine = [[jnp.broadcast_to(e_ref[o, k : k + 1], (8, 128)) for k in range(3)] for o in own]
        sums = (jnp.zeros((8, 128), F), jnp.zeros((8, 128), F))
        for r in range(a, a + 3):
            low = starts[r][b]
            trips = (starts[r][b + 3] - low + (DENS_UNROLL - 1)) // DENS_UNROLL

            def body(t, sums, low=low, mine=mine):
                sums = list(sums)
                for u in range(DENS_UNROLL):
                    g = low + t * DENS_UNROLL + u
                    other = [j_ref[k, g] for k in range(4)]
                    for z in (0, 1):
                        dx, dy, dz = [mine[z][k] - other[k] for k in range(3)]
                        d2 = dx * dx + dy * dy + dz * dz
                        q = d2 * lax.rsqrt(jnp.maximum(d2, 1e-30))
                        outer = jnp.maximum(2.0 - q, 0.0)
                        inner = jnp.maximum(1.0 - q, 0.0)
                        w = 0.25 * (outer * outer * outer) - inner * inner * inner
                        sums[z] = sums[z] + w * other[3]
                return tuple(sums)

            sums = lax.fori_loop(0, trips, body, sums)
        for z in (0, 1):
            rho = jnp.sum(sums[z], axis=0, keepdims=True) * SIGMA
            rho = jnp.where(e_ref[own[z], 6:7] > 0.0, rho, 1.0)
            rho_ref[2 * n + z : 2 * n + z + 1, :] = rho


def force_kernel(
    own_ref, up_ref, right_ref, rho_ref, down_ref, left_ref,
    dens_ref, acc_ref, heat_ref, e_ref, f_ref, c_ref, t_ref, j_ref,
):
    for r in range(4):
        for s in range(4):
            for z in range(2):
                if r == 0:
                    tile = left_ref[2 * s + z]
                elif s == 0:
                    tile = down_ref[2 * (r - 1) + z]
                elif r == 3:
                    tile = right_ref[0, s - 1, z]
                elif s == 3:
                    tile = up_ref[r - 1, 0, z]
                else:
                    tile = own_ref[r - 1, s - 1, z]
                place(e_ref, cell_id(r, s, z), tile, r, s, z)
    for a, b in TARGETS:
        n = 2 * (2 * a + b)
        for source, r, s in (
            (rho_ref[n : n + 2], 2 + a, 2 + b),
            (down_ref[6, n : n + 2], 2 + a, b),
            (left_ref[8, n : n + 2], a, 2 + b),
            (left_ref[9, n : n + 2], a, b),
        ):
            c = cell_id(r, s, 0)
            f_ref[c : c + 2, :] = source
    energy = e_ref[:, 7, :]
    rho = f_ref[...]
    c_ref[0] = (2.0 / 3.0) * energy / rho
    c_ref[1] = 0.25 * jnp.sqrt((10.0 / 9.0) * energy)
    c_ref[2] = 0.25 * rho

    def tile_of(c):
        rows = [e_ref[c]] + [c_ref[k, c : c + 1, :] for k in range(3)] + [jnp.zeros((5, 128), F)]
        return jnp.concatenate(rows, axis=0)

    groups = cell_counts(e_ref)
    starts, total = pack(
        groups, tile_of, t_ref, FORCE_UNROLL,
        pad_tile((1e3, 1e3, 1e3, 0, 0, 0, 0, 0, 0, 0, 0.25, 0, 0, 0, 0, 0)),
    )
    spread(t_ref, j_ref, total, (0, 1, 2, 3, 4, 5, 6, 8, 9, 10))
    for a, b in TARGETS:
        own = [cell_id(1 + a, 1 + b, z) for z in (0, 1)]
        mine = [
            [jnp.broadcast_to(e_ref[o, k : k + 1], (8, 128)) for k in range(6)]
            + [jnp.broadcast_to(c_ref[k, o : o + 1, :], (8, 128)) for k in range(3)]
            for o in own
        ]
        sums = tuple(jnp.zeros((8, 128), F) for _ in range(10))
        for r in range(a, a + 3):
            low = starts[r][b]
            trips = (starts[r][b + 3] - low + (FORCE_UNROLL - 1)) // FORCE_UNROLL

            def body(t, sums, low=low, mine=mine):
                sums = list(sums)
                for u in range(FORCE_UNROLL):
                    g = low + t * FORCE_UNROLL + u
                    J = [j_ref[k, g] for k in range(10)]
                    for z in (0, 1):
                        I = mine[z]
                        dx, dy, dz = [I[k] - J[k] for k in range(3)]
                        d2 = dx * dx + dy * dy + dz * dz
                        vx = (I[3] - J[3]) * dx + (I[4] - J[4]) * dy + (I[5] - J[5]) * dz
                        rs = lax.rsqrt(jnp.maximum(d2, 1e-30))
                        q = d2 * rs
                        outer = jnp.maximum(2.0 - q, 0.0)
                        slope = jnp.where(q < 1.0, 4.0 - 3.0 * q, outer * outer * rs)
                        weight = slope * J[6]
                        closing = jnp.minimum(vx, 0.0)
                        soft = d2 + 0.01
                        visc = (
                            closing * (closing - (I[7] + J[8]) * soft)
                            / (soft * soft * (I[8] + J[9]))
                        )
                        push = weight * (I[6] + J[7] + visc)
                        sums[5 * z] += push * dx
                        sums[5 * z + 1] += push * dy
                        sums[5 * z + 2] += push * dz
                        work = weight * vx
                        sums[5 * z + 3] += work
                        sums[5 * z + 4] += work * visc
                return tuple(sums)

            sums = lax.fori_loop(0, trips, body, sums)
        for z in (0, 1):
            c = own[z]
            filled = jnp.where(e_ref[c, 6:7] > 0.0, 1.0, 0.0)
            scale = filled * (1.5 * SIGMA)
            s = [jnp.sum(sums[5 * z + k], axis=0, keepdims=True) * scale for k in range(5)]
            for k in range(3):
                acc_ref[k, a, b, z : z + 1, :] = s[k]
            heat_ref[a, b, z : z + 1, :] = -(c_ref[0, c : c + 1, :] * s[3] + 0.5 * s[4])
            dens_ref[a, b, z : z + 1, :] = f_ref[c : c + 1, :] * filled


VMEM = pl.BlockSpec(memory_space=pltpu.VMEM)


def shift(block, axis, step):
    count = lax.axis_size(axis)
    return lax.ppermute(block, axis, [((i + step) % count, i) for i in range(count)])


def shards(offsets, velocity, mass, energy, counts):
    slot = lax.broadcasted_iota(jnp.int32, (1, 1, 1, 128), 3)
    filled = (slot < counts[..., None]).astype(F)
    own = jnp.concatenate([offsets, velocity, (mass * filled)[None], energy[None]], axis=0)
    own = jnp.moveaxis(own, 0, 3)
    up = shift(own, "gy", 1)
    right = shift(jnp.concatenate([own, up], axis=1), "gx", 1)
    rho = pl.pallas_call(
        density_kernel,
        name="density",
        out_shape=jax.ShapeDtypeStruct((8, 128), F),
        in_specs=[VMEM] * 3,
        out_specs=VMEM,
        scratch_shapes=[
            pltpu.VMEM((32, 8, 128), F),
            pltpu.VMEM((GROUPS, 8, 128), F),
            pltpu.VMEM((4, GROUPS, 8, 128), F),
        ],
    )(own, up, right)
    cols = [own[0, 1], own[1, 1], right[0, 1], rho[None]]
    down = shift(jnp.concatenate(cols, axis=0), "gy", -1)
    cols = [down[2:4], own[1].reshape(4, 8, 128), up[1, 0], rho[None], down[6:7]]
    left = shift(jnp.concatenate(cols, axis=0), "gx", -1)
    return pl.pallas_call(
        force_kernel,
        name="force",
        out_shape=(
            jax.ShapeDtypeStruct((2, 2, 2, 128), F),
            jax.ShapeDtypeStruct((3, 2, 2, 2, 128), F),
            jax.ShapeDtypeStruct((2, 2, 2, 128), F),
        ),
        in_specs=[VMEM] * 6,
        out_specs=(VMEM, VMEM, VMEM),
        scratch_shapes=[
            pltpu.VMEM((32, 8, 128), F),
            pltpu.VMEM((32, 128), F),
            pltpu.VMEM((3, 32, 128), F),
            pltpu.VMEM((GROUPS, 8, 128), F),
            pltpu.VMEM((10, GROUPS, 8, 128), F),
        ],
    )(own, up, right, rho, down, left)


def solution(mesh):
    in_specs = (
        P(None, "gx", "gy", None, None),
        P(None, "gx", "gy", None, None),
        P("gx", "gy", None, None),
        P("gx", "gy", None, None),
        P("gx", "gy", None),
    )
    out_specs = (
        P("gx", "gy", None, None),
        P(None, "gx", "gy", None, None),
        P("gx", "gy", None, None),
    )
    return jax.shard_map(shards, mesh=mesh, in_specs=in_specs, out_specs=out_specs, check_vma=False)
```

```python
import functools
import math

import jax
import jax.numpy as jnp
from jax import lax
from jax.experimental import pallas as pl
from jax.experimental.pallas import tpu as pltpu
from jax.sharding import PartitionSpec as P

F = jnp.float32
SIGMA = 8.0 / math.pi
DENS_UNROLL = 8
FORCE_UNROLL = 4
CHUNK = 32
GROUPS = 2 * 128 + 2 * 8 + CHUNK + 16
MIB = 1 << 20


def cell_id(r, s, z):
    return (r * 4 + s) * 2 + z


def place(e_ref, c, tile, bx, by, bz):
    row = lax.broadcasted_iota(jnp.int32, (8, 128), 0)
    base = jnp.where(row == 0, F(bx), jnp.where(row == 1, F(by), F(bz)))
    e_ref[c] = jnp.where(row < 3, 2.0 * (tile + base), tile)


def cell_counts(e_ref, first, last):
    masses = e_ref[8 * first : 8 * last, 6, :]
    filled = jnp.sum(jnp.where(masses > 0.0, 1.0, 0.0), axis=1, keepdims=True)
    groups = lax.shift_right_logical(filled.astype(jnp.int32) + 7, 3)
    return {8 * first + c: groups[c, 0] for c in range(8 * (last - first))}


def starts_of(groups, rows, unroll):
    starts = {}
    base = jnp.int32(0)
    for r in rows:
        row = []
        for s in range(4):
            row.append(base)
            base = base + groups[cell_id(r, s, 0)] + groups[cell_id(r, s, 1)]
        row.append(base)
        base = base + (unroll - 1)
        starts[r] = row
    return starts, base


def parts(tile):
    high = tile.astype(jnp.bfloat16).astype(F)
    rest = tile - high
    middle = rest.astype(jnp.bfloat16).astype(F)
    return jnp.concatenate([high, middle, rest - middle], axis=0)


def pad_tile(values):
    lane = lax.broadcasted_iota(jnp.int32, (8, 3 * len(values)), 1)
    tile = jnp.zeros((8, 3 * len(values)), F)
    for k, value in enumerate(values):
        if value:
            tile = jnp.where(lane == k, F(value), tile)
    return tile


def pack(groups, rows, tile_of, t_ref, unroll, pad):
    starts, total = starts_of(groups, rows, unroll)
    clear(t_ref)
    width = pad.shape[1]
    for r in rows:
        for s in range(4):
            base = starts[r][s]
            for z in range(2):
                c = cell_id(r, s, z)
                turned = parts(tile_of(c)).T
                for g in range(16):
                    t_ref[base + g, :, 0:width] = turned[8 * g : 8 * g + 8, :]
                base = base + groups[c]
        for g in range(unroll - 1):
            t_ref[starts[r][4] + g, :, 0:width] = pad
    return starts, total


def clear(t_ref):
    def body(i, carry):
        t_ref[pl.ds(i * CHUNK, CHUNK)] = jnp.zeros((CHUNK, 8, 128), F)
        return carry

    lax.fori_loop(0, GROUPS // CHUNK, body, 0)


def spread(t_ref, j_ref, total, attrs, height):
    row = lax.broadcasted_iota(jnp.int32, (128, 128), 0)
    picks = []
    for k in attrs:
        hit = (row == k) | (row == height + k) | (row == 2 * height + k)
        picks.append(jnp.where(hit, 1.0, 0.0).astype(jnp.bfloat16))
    pick = jnp.concatenate(picks, axis=1)

    def body(i, carry):
        pieces = t_ref[pl.ds(i * CHUNK, CHUNK)].reshape(CHUNK * 8, 128).astype(jnp.bfloat16)
        wide = jnp.dot(pieces, pick, preferred_element_type=F)
        for n in range(len(attrs)):
            j_ref[n, pl.ds(i * CHUNK, CHUNK)] = wide[:, 128 * n : 128 * n + 128].reshape(CHUNK, 8, 128)
        return carry

    lax.fori_loop(0, (total + CHUNK - 1) // CHUNK, body, 0)


def rows_of(ref, c, count):
    return [jnp.broadcast_to(ref[c, k : k + 1], (8, 128)) for k in range(count)]


def density_loop(j_ref, low, high, mine, sums):
    trips = (high - low + (DENS_UNROLL - 1)) // DENS_UNROLL

    def body(t, sums):
        sums = list(sums)
        for u in range(DENS_UNROLL):
            g = low + t * DENS_UNROLL + u
            other = [j_ref[k, g] for k in range(4)]
            for z in (0, 1):
                dx, dy, dz = [mine[z][k] - other[k] for k in range(3)]
                d2 = dx * dx + dy * dy + dz * dz
                q = d2 * lax.rsqrt(jnp.maximum(d2, 1e-30))
                outer = jnp.maximum(2.0 - q, 0.0)
                inner = jnp.maximum(1.0 - q, 0.0)
                w = 0.25 * (outer * outer * outer) - inner * inner * inner
                sums[z] = sums[z] + w * other[3]
        return tuple(sums)

    return lax.fori_loop(0, trips, body, sums)


def force_loop(j_ref, low, high, mine, sums):
    trips = (high - low + (FORCE_UNROLL - 1)) // FORCE_UNROLL

    def body(t, sums):
        sums = list(sums)
        for u in range(FORCE_UNROLL):
            g = low + t * FORCE_UNROLL + u
            J = [j_ref[k, g] for k in range(10)]
            for z in (0, 1):
                I = mine[z]
                dx, dy, dz = [I[k] - J[k] for k in range(3)]
                d2 = dx * dx + dy * dy + dz * dz
                vx = (I[3] - J[3]) * dx + (I[4] - J[4]) * dy + (I[5] - J[5]) * dz
                rs = lax.rsqrt(jnp.maximum(d2, 1e-30))
                q = d2 * rs
                outer = jnp.maximum(2.0 - q, 0.0)
                slope = jnp.where(q < 1.0, 4.0 - 3.0 * q, outer * outer * rs)
                weight = slope * J[6]
                mu = jnp.minimum(vx, 0.0) / (d2 + 0.01)
                visc = mu * (mu - (I[7] + J[8])) / (I[8] + J[9])
                push = weight * (I[6] + J[7] + visc)
                sums[5 * z] += push * dx
                sums[5 * z + 1] += push * dy
                sums[5 * z + 2] += push * dz
                work = weight * vx
                sums[5 * z + 3] += work
                sums[5 * z + 4] += work * visc
        return tuple(sums)

    return lax.fori_loop(0, trips, body, sums)


def zeros(count):
    return tuple(jnp.zeros((8, 128), F) for _ in range(count))


def prepare_kernel(
    counts_hbm, offsets_hbm, velocity_hbm, mass_hbm, energy_hbm, own_ref,
    counts_ref, off, vel, mass, energy, sems,
):
    pairs = [(counts_hbm, counts_ref), (offsets_hbm, off), (velocity_hbm, vel)]
    pairs += [(mass_hbm, mass), (energy_hbm, energy)]
    copies = [pltpu.make_async_copy(a, b, sems.at[i]) for i, (a, b) in enumerate(pairs)]
    for copy in copies:
        copy.start()
    for copy in copies:
        copy.wait()
    slot = lax.broadcasted_iota(jnp.int32, (1, 128), 1)
    for a in range(2):
        for b in range(2):
            for z in range(2):
                for k in range(3):
                    own_ref[a, b, z, k : k + 1, :] = off[k, a, b, z : z + 1, :]
                    own_ref[a, b, z, 3 + k : 4 + k, :] = vel[k, a, b, z : z + 1, :]
                own_ref[a, b, z, 6:7, :] = jnp.where(
                    slot < counts_ref[a, b, z], mass[a, b, z : z + 1, :], 0.0
                )
                own_ref[a, b, z, 7:8, :] = energy[a, b, z : z + 1, :]


DENS_PAD = (1e3, 1e3, 1e3, 0, 0, 0, 0, 0)
DENS_ATTRS = (0, 1, 2, 6)
FORCE_PAD = (1e3, 1e3, 1e3, 0, 0, 0, 0, 0, 0, 0, 0.25, 0, 0, 0, 0, 0)
FORCE_ATTRS = (0, 1, 2, 3, 4, 5, 6, 8, 9, 10)


def density_first(own_ref, up_ref, sums_ref, j_ref, e_ref, t_ref):
    for r in (0, 1):
        for s in range(4):
            for z in range(2):
                tile = up_ref[r, s - 2, z] if s >= 2 else own_ref[r, s, z]
                place(e_ref, cell_id(r, s, z), tile, r - 2, s - 2, z - 1)
    groups = cell_counts(e_ref, 0, 2)
    starts, total = pack(groups, (0, 1), lambda c: e_ref[c], t_ref, DENS_UNROLL, pad_tile(DENS_PAD))
    spread(t_ref, j_ref, total, DENS_ATTRS, 8)
    for b in (0, 1):
        mine = [rows_of(e_ref, cell_id(1, 1 + b, z), 3) for z in (0, 1)]
        sums = zeros(2)
        for r in (0, 1):
            sums = density_loop(j_ref, starts[r][b], starts[r][b + 3], mine, sums)
        for z in (0, 1):
            sums_ref[2 * b + z] = sums[z]


def density_last(own_ref, up_ref, right_ref, sums_ref, j0_ref, message_ref, e_ref, t_ref, j_ref):
    for r in range(4):
        for s in range(4):
            for z in range(2):
                if r >= 2:
                    tile = right_ref[r - 2, s, z]
                else:
                    tile = up_ref[r, s - 2, z] if s >= 2 else own_ref[r, s, z]
                place(e_ref, cell_id(r, s, z), tile, r - 2, s - 2, z - 1)
    groups = cell_counts(e_ref, 0, 4)
    before, _ = starts_of(groups, (0, 1), DENS_UNROLL)
    starts, total = pack(groups, (2, 3), lambda c: e_ref[c], t_ref, DENS_UNROLL, pad_tile(DENS_PAD))
    spread(t_ref, j_ref, total, DENS_ATTRS, 8)
    for a in (0, 1):
        for b in (0, 1):
            own = [cell_id(1 + a, 1 + b, z) for z in (0, 1)]
            mine = [rows_of(e_ref, o, 3) for o in own]
            if a == 0:
                sums = tuple(sums_ref[2 * b + z] for z in (0, 1))
            else:
                sums = zeros(2)
                sums = density_loop(j0_ref, before[1][b], before[1][b + 3], mine, sums)
            for r in (2,) if a == 0 else (2, 3):
                sums = density_loop(j_ref, starts[r][b], starts[r][b + 3], mine, sums)
            for z in (0, 1):
                rho = jnp.sum(sums[z], axis=0, keepdims=True) * SIGMA
                rho = jnp.where(e_ref[own[z], 6:7] > 0.0, rho, 1.0)
                n = 2 * (2 * a + b) + z
                message_ref[6, n : n + 1, :] = rho
    for z in (0, 1):
        message_ref[z] = own_ref[0, 1, z]
        message_ref[2 + z] = own_ref[1, 1, z]
        message_ref[4 + z] = right_ref[0, 1, z]


def force_tiles(rows, own_ref, up_ref, right_ref, sent_ref, down_ref, left_ref, e_ref, f_ref, c_ref):
    for r in rows:
        for s in range(4):
            y = 2 - s
            c = cell_id(r, s, 0)
            for z in range(2):
                if r == 0:
                    tile = left_ref[2 * (y + 1) + z]
                elif y == -1:
                    tile = down_ref[2 * (r - 1) + z]
                elif r == 3:
                    tile = right_ref[0, y, z]
                elif y == 2:
                    tile = up_ref[r - 1, 0, z]
                else:
                    tile = own_ref[r - 1, y, z]
                place(e_ref, c + z, tile, r - 2, y - 1, z - 1)
            n = 2 * (2 * (r % 2) + (y + 1) % 2)
            if r >= 2:
                source = sent_ref[6, n : n + 2] if y >= 1 else down_ref[6, n : n + 2]
            else:
                source = left_ref[8 if y >= 1 else 9, n : n + 2]
            f_ref[c : c + 2, :] = source
    low, high = 8 * rows[0], 8 * rows[-1] + 8
    energy = e_ref[low:high, 7, :]
    rho = f_ref[low:high]
    c_ref[0, low:high] = (2.0 / 3.0) * energy / rho
    c_ref[1, low:high] = 0.25 * jnp.sqrt((10.0 / 9.0) * energy)
    c_ref[2, low:high] = 0.25 * rho


def force_pack(groups, rows, e_ref, c_ref, t_ref, j_ref):
    def tile_of(c):
        rows = [e_ref[c]] + [c_ref[k, c : c + 1, :] for k in range(3)] + [jnp.zeros((5, 128), F)]
        return jnp.concatenate(rows, axis=0)

    starts, total = pack(groups, rows, tile_of, t_ref, FORCE_UNROLL, pad_tile(FORCE_PAD))
    spread(t_ref, j_ref, total, FORCE_ATTRS, 16)
    return starts


def force_rows(e_ref, c_ref, c):
    extra = [jnp.broadcast_to(c_ref[k, c : c + 1, :], (8, 128)) for k in range(3)]
    return rows_of(e_ref, c, 6) + extra


def force_first(
    own_ref, up_ref, right_ref, sent_ref, down_ref, sums_ref, j_ref, e_ref, f_ref, c_ref, t_ref
):
    rows = (2, 3)
    force_tiles(rows, own_ref, up_ref, right_ref, sent_ref, down_ref, None, e_ref, f_ref, c_ref)
    groups = cell_counts(e_ref, 2, 4)
    starts = force_pack(groups, rows, e_ref, c_ref, t_ref, j_ref)
    for b in (0, 1):
        mine = [force_rows(e_ref, c_ref, cell_id(2, 2 - b, z)) for z in (0, 1)]
        sums = zeros(10)
        for r in rows:
            sums = force_loop(j_ref, starts[r][1 - b], starts[r][4 - b], mine, sums)
        for k in range(10):
            sums_ref[10 * b + k] = sums[k]


def force_last(
    own_ref, up_ref, right_ref, sent_ref, down_ref, left_ref, sums_ref, j0_ref,
    dens_ref, acc_ref, heat_ref, e_ref, f_ref, c_ref, t_ref, j_ref,
):
    rows = (0, 1, 2)
    force_tiles(rows, own_ref, up_ref, right_ref, sent_ref, down_ref, left_ref, e_ref, f_ref, c_ref)
    groups = cell_counts(e_ref, 0, 3)
    before = []
    base = jnp.int32(0)
    for s in range(4):
        before.append(base)
        base = base + groups[cell_id(2, s, 0)] + groups[cell_id(2, s, 1)]
    before.append(base)
    starts = force_pack(groups, (0, 1), e_ref, c_ref, t_ref, j_ref)
    for a in (0, 1):
        for b in (0, 1):
            own = [cell_id(1 + a, 2 - b, z) for z in (0, 1)]
            mine = [force_rows(e_ref, c_ref, o) for o in own]
            if a == 0:
                sums = zeros(10)
                sums = force_loop(j0_ref, before[1 - b], before[4 - b], mine, sums)
            else:
                sums = tuple(sums_ref[10 * b + k] for k in range(10))
            for r in (0, 1) if a == 0 else (1,):
                sums = force_loop(j_ref, starts[r][1 - b], starts[r][4 - b], mine, sums)
            for z in (0, 1):
                c = own[z]
                filled = jnp.where(e_ref[c, 6:7] > 0.0, 1.0, 0.0)
                scale = filled * (1.5 * SIGMA)
                s = [jnp.sum(sums[5 * z + k], axis=0, keepdims=True) * scale for k in range(5)]
                for k in range(3):
                    acc_ref[k, a, b, z : z + 1, :] = s[k]
                heat_ref[a, b, z : z + 1, :] = -(c_ref[0, c : c + 1, :] * s[3] + 0.5 * s[4])
                dens_ref[a, b, z : z + 1, :] = f_ref[c : c + 1, :] * filled


VMEM = pl.BlockSpec(memory_space=pltpu.VMEM)
HBM = pl.BlockSpec(memory_space=pltpu.HBM)
SMEM = pl.BlockSpec(memory_space=pltpu.SMEM)


def array(*shape):
    return jax.ShapeDtypeStruct(shape, F)


def call(kernel, name, outs, scratch, limit, flops, in_specs):
    return pl.pallas_call(
        kernel,
        name=name,
        out_shape=outs,
        in_specs=in_specs,
        out_specs=jax.tree.map(lambda _: VMEM, outs),
        scratch_shapes=scratch,
        cost_estimate=pl.CostEstimate(flops=flops, bytes_accessed=1 << 18, transcendentals=0),
        compiler_params=pltpu.CompilerParams(vmem_limit_bytes=limit * MIB),
    )


def shift(block, axis, step):
    count = lax.axis_size(axis)
    return lax.ppermute(block, axis, [((i + step) % count, i) for i in range(count)])


def shards(offsets, velocity, mass, energy, counts):
    tiles = pltpu.VMEM((32, 8, 128), F)
    packed = pltpu.VMEM((GROUPS, 8, 128), F)
    vector = pltpu.VMEM((3, 2, 2, 2, 128), F)
    scalar = pltpu.VMEM((2, 2, 2, 128), F)
    own = call(
        prepare_kernel, "prepare", array(2, 2, 2, 8, 128),
        [pltpu.SMEM((2, 2, 2), jnp.int32), vector, vector, scalar, scalar, pltpu.SemaphoreType.DMA((5,))],
        8, 1 << 16, [HBM] * 5,
    )(*[pltpu.with_memory_space_constraint(v, pltpu.HBM) for v in (counts, offsets, velocity, mass, energy)])
    up = shift(own, "gy", 1)
    right = shift(jnp.concatenate([own, up], axis=1), "gx", 1)
    sums, spread_first = call(
        density_first, "density_first", (array(4, 8, 128), array(4, GROUPS, 8, 128)),
        [tiles, packed], 12, 1 << 27, [VMEM] * 2,
    )(own, up)
    sent = call(
        density_last, "density_last", array(7, 8, 128),
        [tiles, packed, pltpu.VMEM((4, GROUPS, 8, 128), F)], 16, 1 << 27, [VMEM] * 5,
    )(own, up, right, sums, spread_first)
    down = shift(sent, "gy", -1)
    cols = [down[2:4], own[1].reshape(4, 8, 128), up[1, 0], sent[6:7], down[6:7]]
    left = shift(jnp.concatenate(cols, axis=0), "gx", -1)
    more = [pltpu.VMEM((32, 128), F), pltpu.VMEM((3, 32, 128), F)]
    sums, spread_first = call(
        force_first, "force_first", (array(20, 8, 128), array(10, GROUPS, 8, 128)),
        [tiles] + more + [packed], 20, 1 << 28, [VMEM] * 5,
    )(own, up, right, sent, down)
    return call(
        force_last, "force_last", (array(2, 2, 2, 128), array(3, 2, 2, 2, 128), array(2, 2, 2, 128)),
        [tiles] + more + [packed, pltpu.VMEM((10, GROUPS, 8, 128), F)], 24, 1 << 28, [VMEM] * 8,
    )(own, up, right, sent, down, left, sums, spread_first)


def solution(mesh):
    in_specs = (
        P(None, "gx", "gy", None, None),
        P(None, "gx", "gy", None, None),
        P("gx", "gy", None, None),
        P("gx", "gy", None, None),
        P("gx", "gy", None),
    )
    out_specs = (
        P("gx", "gy", None, None),
        P(None, "gx", "gy", None, None),
        P("gx", "gy", None, None),
    )
    return jax.shard_map(shards, mesh=mesh, in_specs=in_specs, out_specs=out_specs, check_vma=False)
```

```python
import functools
import math

import jax
import jax.numpy as jnp
from jax import lax
from jax.experimental import pallas as pl
from jax.experimental.pallas import tpu as pltpu
from jax.sharding import PartitionSpec as P

F = jnp.float32
SIGMA = 8.0 / math.pi
DENS_UNROLL = 8
FORCE_UNROLL = 4
CHUNK = 32
GROUPS = 320
HALF = 160
MIB = 1 << 20


def cell_id(r, s, z):
    return (r * 4 + s) * 2 + z


def place(e_ref, c, tile, bx, by, bz):
    row = lax.broadcasted_iota(jnp.int32, (8, 128), 0)
    base = jnp.where(row == 0, F(-1 - bx), jnp.where(row == 1, F(-1 - by), F(bz)))
    e_ref[c] = jnp.where(row < 3, 2.0 * (tile + base), tile)


def cell_counts(e_ref, first, last):
    masses = e_ref[8 * first : 8 * last, 6, :]
    filled = jnp.sum(jnp.where(masses > 0.0, 1.0, 0.0), axis=1, keepdims=True)
    groups = lax.shift_right_logical(filled.astype(jnp.int32) + 7, 3)
    return {8 * first + c: groups[c, 0] for c in range(8 * (last - first))}


def lay(groups, runs, unroll):
    starts = []
    base = jnp.int32(0)
    for run in runs:
        row = []
        for r, s in run:
            row.append(base)
            base = base + groups[cell_id(r, s, 0)] + groups[cell_id(r, s, 1)]
        row.append(base)
        base = base + (unroll - 1)
        starts.append(row)
    return starts, base


def parts(tile):
    high = tile.astype(jnp.bfloat16).astype(F)
    rest = tile - high
    middle = rest.astype(jnp.bfloat16).astype(F)
    return jnp.concatenate([high, middle, rest - middle], axis=0)


def pad_tile(values):
    lane = lax.broadcasted_iota(jnp.int32, (8, 3 * len(values)), 1)
    tile = jnp.zeros((8, 3 * len(values)), F)
    for k, value in enumerate(values):
        if value:
            tile = jnp.where(lane == k, F(value), tile)
    return tile


def pack(groups, runs, tile_of, t_ref, unroll, pad):
    starts, total = lay(groups, runs, unroll)
    clear(t_ref)
    width = pad.shape[1]
    for run, row in zip(runs, starts):
        for (r, s), base in zip(run, row):
            for z in range(2):
                c = cell_id(r, s, z)
                turned = parts(tile_of(c)).T
                for g in range(16):
                    t_ref[base + g, :, 0:width] = turned[8 * g : 8 * g + 8, :]
                base = base + groups[c]
        for g in range(unroll - 1):
            t_ref[row[-1] + g, :, 0:width] = pad
    return starts, total


def full(r):
    return [(r, s) for s in range(4)]


def clear(t_ref):
    def body(i, carry):
        t_ref[pl.ds(i * CHUNK, CHUNK)] = jnp.zeros((CHUNK, 8, 128), F)
        return carry

    lax.fori_loop(0, t_ref.shape[0] // CHUNK, body, 0)


def spread(t_ref, j_ref, total, attrs, height):
    row = lax.broadcasted_iota(jnp.int32, (128, 128), 0)
    picks = []
    for k in attrs:
        hit = (row == k) | (row == height + k) | (row == 2 * height + k)
        picks.append(jnp.where(hit, 1.0, 0.0).astype(jnp.bfloat16))
    pick = jnp.concatenate(picks, axis=1)

    def body(i, carry):
        pieces = t_ref[pl.ds(i * CHUNK, CHUNK)].reshape(CHUNK * 8, 128).astype(jnp.bfloat16)
        wide = jnp.dot(pieces, pick, preferred_element_type=F)
        for n in range(len(attrs)):
            j_ref[n, pl.ds(i * CHUNK, CHUNK)] = wide[:, 128 * n : 128 * n + 128].reshape(CHUNK, 8, 128)
        return carry

    lax.fori_loop(0, (total + CHUNK - 1) // CHUNK, body, 0)


def rows_of(ref, c, count):
    return [jnp.broadcast_to(ref[c, k : k + 1], (8, 128)) for k in range(count)]


def density_loop(j_ref, low, high, mine, sums):
    trips = (high - low + (DENS_UNROLL - 1)) // DENS_UNROLL

    def body(t, sums):
        sums = list(sums)
        for u in range(DENS_UNROLL):
            g = low + t * DENS_UNROLL + u
            other = [j_ref[k, g] for k in range(4)]
            for z in (0, 1):
                dx, dy, dz = [mine[z][k] - other[k] for k in range(3)]
                d2 = dx * dx + dy * dy + dz * dz
                q = d2 * lax.rsqrt(jnp.maximum(d2, 1e-30))
                outer = jnp.maximum(2.0 - q, 0.0)
                inner = jnp.maximum(1.0 - q, 0.0)
                w = 0.25 * (outer * outer * outer) - inner * inner * inner
                sums[z] = sums[z] + w * other[3]
        return tuple(sums)

    return lax.fori_loop(0, trips, body, sums)


def force_loop(j_ref, low, high, mine, sums):
    trips = (high - low + (FORCE_UNROLL - 1)) // FORCE_UNROLL

    def body(t, sums):
        sums = list(sums)
        for u in range(FORCE_UNROLL):
            g = low + t * FORCE_UNROLL + u
            J = [j_ref[k, g] for k in range(10)]
            for z in (0, 1):
                I = mine[z]
                dx, dy, dz = [I[k] - J[k] for k in range(3)]
                d2 = dx * dx + dy * dy + dz * dz
                vx = (I[3] - J[3]) * dx + (I[4] - J[4]) * dy + (I[5] - J[5]) * dz
                rs = lax.rsqrt(jnp.maximum(d2, 1e-30))
                q = d2 * rs
                outer = jnp.maximum(2.0 - q, 0.0)
                slope = jnp.where(q < 1.0, 4.0 - 3.0 * q, outer * outer * rs)
                weight = slope * J[6]
                mu = jnp.minimum(vx, 0.0) / (d2 + 0.01)
                visc = mu * (mu - (I[7] + J[8])) / (I[8] + J[9])
                push = weight * (I[6] + J[7] + visc)
                sums[5 * z] += push * dx
                sums[5 * z + 1] += push * dy
                sums[5 * z + 2] += push * dz
                work = weight * vx
                sums[5 * z + 3] += work
                sums[5 * z + 4] += work * visc
        return tuple(sums)

    return lax.fori_loop(0, trips, body, sums)


def zeros(count):
    return tuple(jnp.zeros((8, 128), F) for _ in range(count))


def prepare_kernel(
    counts_hbm, offsets_hbm, velocity_hbm, mass_hbm, energy_hbm, own_ref,
    counts_ref, off, vel, mass, energy, sems,
):
    pairs = [(counts_hbm, counts_ref), (offsets_hbm, off), (velocity_hbm, vel)]
    pairs += [(mass_hbm, mass), (energy_hbm, energy)]
    copies = [pltpu.make_async_copy(a, b, sems.at[i]) for i, (a, b) in enumerate(pairs)]
    for copy in copies:
        copy.start()
    for copy in copies:
        copy.wait()
    slot = lax.broadcasted_iota(jnp.int32, (1, 128), 1)
    for a in range(2):
        for b in range(2):
            for z in range(2):
                for k in range(3):
                    own_ref[1 - a, 1 - b, z, k : k + 1, :] = off[k, a, b, z : z + 1, :]
                    own_ref[1 - a, 1 - b, z, 3 + k : 4 + k, :] = vel[k, a, b, z : z + 1, :]
                own_ref[1 - a, 1 - b, z, 6:7, :] = jnp.where(
                    slot < counts_ref[a, b, z], mass[a, b, z : z + 1, :], 0.0
                )
                own_ref[1 - a, 1 - b, z, 7:8, :] = energy[a, b, z : z + 1, :]


DENS_PAD = (1e3, 1e3, 1e3, 0, 0, 0, 0, 0)
DENS_ATTRS = (0, 1, 2, 6)
FORCE_PAD = (1e3, 1e3, 1e3, 0, 0, 0, 0, 0, 0, 0, 0.25, 0, 0, 0, 0, 0)
FORCE_ATTRS = (0, 1, 2, 3, 4, 5, 6, 8, 9, 10)


NEAR = [[(1, 0), (1, 1)], [(0, 0), (0, 1)]]
AHEAD = [[(1, 2), (1, 3)], [(0, 2), (0, 3)]]


def density_tiles(columns, own_ref, up_ref, right_ref, e_ref):
    for r, s in columns:
        for z in range(2):
            if r >= 2:
                tile = right_ref[r - 2, s, z]
            else:
                tile = up_ref[r, s - 2, z] if s >= 2 else own_ref[r, s, z]
            place(e_ref, cell_id(r, s, z), tile, r - 2, s - 2, z - 1)


def density_pack(groups, runs, e_ref, t_ref, j_ref):
    pad = pad_tile(DENS_PAD)
    starts, total = pack(groups, runs, lambda c: e_ref[c], t_ref, DENS_UNROLL, pad)
    spread(t_ref, j_ref, total, DENS_ATTRS, 8)
    return starts


def density_own(own_ref, sums_ref, j_ref, e_ref, t_ref):
    density_tiles(NEAR[0] + NEAR[1], own_ref, None, None, e_ref)
    starts = density_pack(cell_counts(e_ref, 0, 2), NEAR, e_ref, t_ref, j_ref)
    mine = [rows_of(e_ref, cell_id(1, 1, z), 3) for z in (0, 1)]
    sums = zeros(2)
    for row in starts:
        sums = density_loop(j_ref, row[0], row[2], mine, sums)
    for z in (0, 1):
        sums_ref[z] = sums[z]


def density_first(own_ref, up_ref, part_ref, jn_ref, sums_ref, j_ref, e_ref, t_ref):
    density_tiles(full(0) + full(1), own_ref, up_ref, None, e_ref)
    groups = cell_counts(e_ref, 0, 2)
    near, _ = lay(groups, NEAR, DENS_UNROLL)
    starts = density_pack(groups, AHEAD, e_ref, t_ref, j_ref)
    for b in (0, 1):
        mine = [rows_of(e_ref, cell_id(1, 1 + b, z), 3) for z in (0, 1)]
        sums = zeros(2) if b else tuple(part_ref[z] for z in (0, 1))
        for i in (0, 1):
            if b:
                sums = density_loop(jn_ref, near[i][1], near[i][2], mine, sums)
            sums = density_loop(j_ref, starts[i][0], starts[i][1 + b], mine, sums)
        for z in (0, 1):
            sums_ref[2 * b + z] = sums[z]


def density_last(
    own_ref, up_ref, right_ref, sums_ref, jn_ref, ja_ref, message_ref, e_ref, t_ref, j_ref
):
    density_tiles(full(1) + full(2) + full(3), own_ref, up_ref, right_ref, e_ref)
    groups = cell_counts(e_ref, 1, 4)
    near = lay(groups, NEAR[:1], DENS_UNROLL)[0][0]
    ahead = lay(groups, AHEAD[:1], DENS_UNROLL)[0][0]
    starts = density_pack(groups, [full(2), full(3)], e_ref, t_ref, j_ref)
    for a in (0, 1):
        for b in (0, 1):
            own = [cell_id(1 + a, 1 + b, z) for z in (0, 1)]
            mine = [rows_of(e_ref, o, 3) for o in own]
            if a == 0:
                sums = tuple(sums_ref[2 * b + z] for z in (0, 1))
            else:
                sums = zeros(2)
                sums = density_loop(jn_ref, near[b], near[2], mine, sums)
                sums = density_loop(ja_ref, ahead[0], ahead[1 + b], mine, sums)
            for i in (0,) if a == 0 else (0, 1):
                sums = density_loop(j_ref, starts[i][b], starts[i][b + 3], mine, sums)
            for z in (0, 1):
                rho = jnp.sum(sums[z], axis=0, keepdims=True) * SIGMA
                rho = jnp.where(e_ref[own[z], 6:7] > 0.0, rho, 1.0)
                n = 2 * (2 * a + b) + z
                message_ref[6, n : n + 1, :] = rho
    for z in (0, 1):
        message_ref[z] = own_ref[0, 1, z]
        message_ref[2 + z] = own_ref[1, 1, z]
        message_ref[4 + z] = right_ref[0, 1, z]


def force_tiles(columns, own_ref, up_ref, right_ref, sent_ref, down_ref, left_ref, e_ref, f_ref, c_ref):
    for r, s in columns:
        y = 2 - s
        c = cell_id(r, s, 0)
        for z in range(2):
            if r == 0:
                tile = left_ref[2 * (y + 1) + z]
            elif y == -1:
                tile = down_ref[2 * (r - 1) + z]
            elif r == 3:
                tile = right_ref[0, y, z]
            elif y == 2:
                tile = up_ref[r - 1, 0, z]
            else:
                tile = own_ref[r - 1, y, z]
            place(e_ref, c + z, tile, r - 2, y - 1, z - 1)
        n = 2 * (2 * (r % 2) + (y + 1) % 2)
        if r >= 2:
            source = sent_ref[6, n : n + 2] if y >= 1 else down_ref[6, n : n + 2]
        else:
            source = left_ref[8 if y >= 1 else 9, n : n + 2]
        f_ref[c : c + 2, :] = source
    low, high = 8 * columns[0][0], 8 * columns[-1][0] + 8
    energy = e_ref[low:high, 7, :]
    rho = f_ref[low:high]
    c_ref[0, low:high] = (2.0 / 3.0) * energy / rho
    c_ref[1, low:high] = 0.25 * jnp.sqrt((10.0 / 9.0) * energy)
    c_ref[2, low:high] = 0.25 * rho


def force_pack(groups, runs, e_ref, c_ref, t_ref, j_ref):
    def tile_of(c):
        rows = [e_ref[c]] + [c_ref[k, c : c + 1, :] for k in range(3)] + [jnp.zeros((5, 128), F)]
        return jnp.concatenate(rows, axis=0)

    starts, total = pack(groups, runs, tile_of, t_ref, FORCE_UNROLL, pad_tile(FORCE_PAD))
    spread(t_ref, j_ref, total, FORCE_ATTRS, 16)
    return starts


def force_rows(e_ref, c_ref, c):
    extra = [jnp.broadcast_to(c_ref[k, c : c + 1, :], (8, 128)) for k in range(3)]
    return rows_of(e_ref, c, 6) + extra


UPPER = [[(2, 0), (2, 1)], [(3, 0), (3, 1)]]
LOWER = [[(2, 2), (2, 3)], [(3, 2), (3, 3)]]


def force_upper(own_ref, up_ref, right_ref, sent_ref, sums_ref, j_ref, e_ref, f_ref, c_ref, t_ref):
    force_tiles(UPPER[0] + UPPER[1], own_ref, up_ref, right_ref, sent_ref, None, None, e_ref, f_ref, c_ref)
    starts = force_pack(cell_counts(e_ref, 2, 4), UPPER, e_ref, c_ref, t_ref, j_ref)
    mine = [force_rows(e_ref, c_ref, cell_id(2, 1, z)) for z in (0, 1)]
    sums = zeros(10)
    for row in starts:
        sums = force_loop(j_ref, row[0], row[2], mine, sums)
    for k in range(10):
        sums_ref[k] = sums[k]


def force_first(
    own_ref, up_ref, right_ref, sent_ref, down_ref, part_ref, ju_ref, sums_ref, j_ref,
    e_ref, f_ref, c_ref, t_ref,
):
    columns = full(2) + full(3)
    force_tiles(columns, own_ref, up_ref, right_ref, sent_ref, down_ref, None, e_ref, f_ref, c_ref)
    groups = cell_counts(e_ref, 2, 4)
    upper, _ = lay(groups, UPPER, FORCE_UNROLL)
    starts = force_pack(groups, LOWER, e_ref, c_ref, t_ref, j_ref)
    for b in (0, 1):
        mine = [force_rows(e_ref, c_ref, cell_id(2, 2 - b, z)) for z in (0, 1)]
        sums = tuple(part_ref[k] for k in range(10)) if b else zeros(10)
        for i in (0, 1):
            if not b:
                sums = force_loop(ju_ref, upper[i][1], upper[i][2], mine, sums)
            sums = force_loop(j_ref, starts[i][0], starts[i][2 - b], mine, sums)
        for k in range(10):
            sums_ref[10 * b + k] = sums[k]


def force_last(
    own_ref, up_ref, right_ref, sent_ref, down_ref, left_ref, sums_ref, ju_ref, jl_ref,
    dens_ref, acc_ref, heat_ref, e_ref, f_ref, c_ref, t_ref, j_ref,
):
    columns = full(0) + full(1) + full(2)
    force_tiles(columns, own_ref, up_ref, right_ref, sent_ref, down_ref, left_ref, e_ref, f_ref, c_ref)
    groups = cell_counts(e_ref, 0, 3)
    upper = lay(groups, UPPER[:1], FORCE_UNROLL)[0][0]
    lower = lay(groups, LOWER[:1], FORCE_UNROLL)[0][0]
    starts = force_pack(groups, [full(0), full(1)], e_ref, c_ref, t_ref, j_ref)
    for a in (0, 1):
        for b in (0, 1):
            own = [cell_id(1 + a, 2 - b, z) for z in (0, 1)]
            mine = [force_rows(e_ref, c_ref, o) for o in own]
            if a == 0:
                sums = zeros(10)
                sums = force_loop(ju_ref, upper[1 - b], upper[2], mine, sums)
                sums = force_loop(jl_ref, lower[0], lower[2 - b], mine, sums)
            else:
                sums = tuple(sums_ref[10 * b + k] for k in range(10))
            for r in (0, 1) if a == 0 else (1,):
                sums = force_loop(j_ref, starts[r][1 - b], starts[r][4 - b], mine, sums)
            for z in (0, 1):
                c = own[z]
                filled = jnp.where(e_ref[c, 6:7] > 0.0, 1.0, 0.0)
                scale = filled * (1.5 * SIGMA)
                s = [jnp.sum(sums[5 * z + k], axis=0, keepdims=True) * scale for k in range(5)]
                for k in range(3):
                    acc_ref[k, 1 - a, 1 - b, z : z + 1, :] = s[k]
                heat_ref[1 - a, 1 - b, z : z + 1, :] = -(c_ref[0, c : c + 1, :] * s[3] + 0.5 * s[4])
                dens_ref[1 - a, 1 - b, z : z + 1, :] = f_ref[c : c + 1, :] * filled


VMEM = pl.BlockSpec(memory_space=pltpu.VMEM)
HBM = pl.BlockSpec(memory_space=pltpu.HBM)
SMEM = pl.BlockSpec(memory_space=pltpu.SMEM)


def array(*shape):
    return jax.ShapeDtypeStruct(shape, F)


def call(kernel, name, outs, scratch, limit, flops, in_specs):
    return pl.pallas_call(
        kernel,
        name=name,
        out_shape=outs,
        in_specs=in_specs,
        out_specs=jax.tree.map(lambda _: VMEM, outs),
        scratch_shapes=scratch,
        cost_estimate=pl.CostEstimate(flops=flops, bytes_accessed=1 << 18, transcendentals=0),
        compiler_params=pltpu.CompilerParams(vmem_limit_bytes=limit * MIB),
    )


def shift(block, axis, step):
    count = lax.axis_size(axis)
    return lax.ppermute(block, axis, [((i + step) % count, i) for i in range(count)])


def shards(offsets, velocity, mass, energy, counts):
    tiles = pltpu.VMEM((32, 8, 128), F)
    packed = pltpu.VMEM((GROUPS, 8, 128), F)
    vector = pltpu.VMEM((3, 2, 2, 2, 128), F)
    scalar = pltpu.VMEM((2, 2, 2, 128), F)
    own = call(
        prepare_kernel, "prepare", array(2, 2, 2, 8, 128),
        [pltpu.SMEM((2, 2, 2), jnp.int32), vector, vector, scalar, scalar, pltpu.SemaphoreType.DMA((5,))],
        8, 1 << 16, [HBM] * 5,
    )(*[pltpu.with_memory_space_constraint(v, pltpu.HBM) for v in (counts, offsets, velocity, mass, energy)])
    half = pltpu.VMEM((HALF, 8, 128), F)
    up = shift(own, "gy", -1)
    part, near = call(
        density_own, "density_own", (array(2, 8, 128), array(4, HALF, 8, 128)),
        [tiles, half], 12, 1 << 26, [VMEM],
    )(own)
    part, up = lax.optimization_barrier((part, up))
    right = shift(jnp.concatenate([own, up], axis=1), "gx", -1)
    sums, ahead = call(
        density_first, "density_first", (array(4, 8, 128), array(4, HALF, 8, 128)),
        [tiles, half], 12, 1 << 27, [VMEM] * 4,
    )(own, up, part, near)
    sent = call(
        density_last, "density_last", array(7, 8, 128),
        [tiles, packed, pltpu.VMEM((4, GROUPS, 8, 128), F)], 16, 1 << 27, [VMEM] * 6,
    )(own, up, right, sums, near, ahead)
    down = shift(sent, "gy", 1)
    more = [tiles, pltpu.VMEM((32, 128), F), pltpu.VMEM((3, 32, 128), F)]
    part, upper = call(
        force_upper, "force_upper", (array(10, 8, 128), array(10, HALF, 8, 128)),
        more + [half], 16, 1 << 27, [VMEM] * 4,
    )(own, up, right, sent)
    part, down = lax.optimization_barrier((part, down))
    cols = [down[2:4], own[1].reshape(4, 8, 128), up[1, 0], sent[6:7], down[6:7]]
    left = shift(jnp.concatenate(cols, axis=0), "gx", 1)
    sums, lower = call(
        force_first, "force_first", (array(20, 8, 128), array(10, HALF, 8, 128)),
        more + [half], 16, 1 << 28, [VMEM] * 7,
    )(own, up, right, sent, down, part, upper)
    return call(
        force_last, "force_last", (array(2, 2, 2, 128), array(3, 2, 2, 2, 128), array(2, 2, 2, 128)),
        more + [packed, pltpu.VMEM((10, GROUPS, 8, 128), F)], 24, 1 << 28, [VMEM] * 9,
    )(own, up, right, sent, down, left, sums, upper, lower)


def solution(mesh):
    in_specs = (
        P(None, "gx", "gy", None, None),
        P(None, "gx", "gy", None, None),
        P("gx", "gy", None, None),
        P("gx", "gy", None, None),
        P("gx", "gy", None),
    )
    out_specs = (
        P("gx", "gy", None, None),
        P(None, "gx", "gy", None, None),
        P("gx", "gy", None, None),
    )
    return jax.shard_map(shards, mesh=mesh, in_specs=in_specs, out_specs=out_specs, check_vma=False)
```

```python
import functools
import math

import jax
import jax.numpy as jnp
from jax import lax
from jax.experimental import pallas as pl
from jax.experimental.pallas import tpu as pltpu
from jax.sharding import PartitionSpec as P

F = jnp.float32
SIGMA = 8.0 / math.pi
DENS_UNROLL = 8
FORCE_UNROLL = 4
CHUNK = 32
GROUPS = 320
HALF = 160
MIB = 1 << 20


def cell_id(r, s, z):
    return (r * 4 + s) * 2 + z


def place(e_ref, c, tile, bx, by, bz):
    row = lax.broadcasted_iota(jnp.int32, (8, 128), 0)
    base = jnp.where(row == 0, F(-1 - bx), jnp.where(row == 1, F(-1 - by), F(bz)))
    e_ref[c] = jnp.where(row < 3, 2.0 * (tile + base), tile)


def cell_counts(e_ref, first, last):
    masses = e_ref[8 * first : 8 * last, 6, :]
    filled = jnp.sum(jnp.where(masses > 0.0, 1.0, 0.0), axis=1, keepdims=True)
    groups = lax.shift_right_logical(filled.astype(jnp.int32) + 7, 3)
    return {8 * first + c: groups[c, 0] for c in range(8 * (last - first))}


def lay(groups, runs, unroll):
    starts = []
    base = jnp.int32(0)
    for run in runs:
        row = []
        for r, s in run:
            row.append(base)
            base = base + groups[cell_id(r, s, 0)] + groups[cell_id(r, s, 1)]
        row.append(base)
        base = base + (unroll - 1)
        starts.append(row)
    return starts, base


def parts(tile):
    high = tile.astype(jnp.bfloat16).astype(F)
    rest = tile - high
    middle = rest.astype(jnp.bfloat16).astype(F)
    return jnp.concatenate([high, middle, rest - middle], axis=0)


def pad_tile(values):
    lane = lax.broadcasted_iota(jnp.int32, (8, 3 * len(values)), 1)
    tile = jnp.zeros((8, 3 * len(values)), F)
    for k, value in enumerate(values):
        if value:
            tile = jnp.where(lane == k, F(value), tile)
    return tile


def pack(groups, runs, tile_of, t_ref, unroll, pad):
    starts, total = lay(groups, runs, unroll)
    width = pad.shape[1]
    for run, row in zip(runs, starts):
        for (r, s), base in zip(run, row):
            for z in range(2):
                c = cell_id(r, s, z)
                turned = parts(tile_of(c)).T
                for g in range(16):
                    t_ref[base + g, :, 0:width] = turned[8 * g : 8 * g + 8, :]
                base = base + groups[c]
        for g in range(unroll - 1):
            t_ref[row[-1] + g, :, 0:width] = pad
    return starts, total


def full(r):
    return [(r, s) for s in range(4)]


def spread(t_ref, j_ref, total, attrs, height):
    row = lax.broadcasted_iota(jnp.int32, (128, 128), 0)
    picks = []
    for k in attrs:
        hit = (row == k) | (row == height + k) | (row == 2 * height + k)
        picks.append(jnp.where(hit, 1.0, 0.0).astype(jnp.bfloat16))
    pick = jnp.concatenate(picks, axis=1)

    def body(i, carry):
        pieces = t_ref[pl.ds(i * CHUNK, CHUNK)].reshape(CHUNK * 8, 128)
        lane = lax.broadcasted_iota(jnp.int32, pieces.shape, 1)
        pieces = jnp.where(lane < 3 * height, pieces, 0.0).astype(jnp.bfloat16)
        wide = jnp.dot(pieces, pick, preferred_element_type=F)
        for n in range(len(attrs)):
            j_ref[n, pl.ds(i * CHUNK, CHUNK)] = wide[:, 128 * n : 128 * n + 128].reshape(CHUNK, 8, 128)
        return carry

    lax.fori_loop(0, (total + CHUNK - 1) // CHUNK, body, 0)


def rows_of(ref, c, count):
    return [jnp.broadcast_to(ref[c, k : k + 1], (8, 128)) for k in range(count)]


def density_loop(j_ref, low, high, mine, sums):
    trips = (high - low + (DENS_UNROLL - 1)) // DENS_UNROLL

    def body(t, sums):
        sums = list(sums)
        for u in range(DENS_UNROLL):
            g = low + t * DENS_UNROLL + u
            other = [j_ref[k, g] for k in range(4)]
            for z in (0, 1):
                dx, dy, dz = [mine[z][k] - other[k] for k in range(3)]
                d2 = dx * dx + dy * dy + dz * dz
                q = d2 * lax.rsqrt(jnp.maximum(d2, 1e-30))
                outer = jnp.maximum(2.0 - q, 0.0)
                inner = jnp.maximum(1.0 - q, 0.0)
                w = 0.25 * (outer * outer * outer) - inner * inner * inner
                sums[z] = sums[z] + w * other[3]
        return tuple(sums)

    return lax.fori_loop(0, trips, body, sums)


def force_loop(j_ref, low, high, mine, sums):
    trips = (high - low + (FORCE_UNROLL - 1)) // FORCE_UNROLL

    def body(t, sums):
        sums = list(sums)
        for u in range(FORCE_UNROLL):
            g = low + t * FORCE_UNROLL + u
            J = [j_ref[k, g] for k in range(10)]
            for z in (0, 1):
                I = mine[z]
                dx, dy, dz = [I[k] - J[k] for k in range(3)]
                d2 = dx * dx + dy * dy + dz * dz
                vx = (I[3] - J[3]) * dx + (I[4] - J[4]) * dy + (I[5] - J[5]) * dz
                rs = lax.rsqrt(jnp.maximum(d2, 1e-30))
                q = d2 * rs
                outer = jnp.maximum(2.0 - q, 0.0)
                slope = jnp.where(q < 1.0, 4.0 - 3.0 * q, outer * outer * rs)
                weight = slope * J[6]
                mu = jnp.minimum(vx, 0.0) / (d2 + 0.01)
                visc = mu * (mu - (I[7] + J[8])) / (I[8] + J[9])
                push = weight * (I[6] + J[7] + visc)
                sums[5 * z] += push * dx
                sums[5 * z + 1] += push * dy
                sums[5 * z + 2] += push * dz
                work = weight * vx
                sums[5 * z + 3] += work
                sums[5 * z + 4] += work * visc
        return tuple(sums)

    return lax.fori_loop(0, trips, body, sums)


def zeros(count):
    return tuple(jnp.zeros((8, 128), F) for _ in range(count))


def prepare_kernel(
    counts_hbm, offsets_hbm, velocity_hbm, mass_hbm, energy_hbm, own_ref,
    counts_ref, off, vel, mass, energy, sems,
):
    pairs = [(counts_hbm, counts_ref), (offsets_hbm, off), (velocity_hbm, vel)]
    pairs += [(mass_hbm, mass), (energy_hbm, energy)]
    copies = [pltpu.make_async_copy(a, b, sems.at[i]) for i, (a, b) in enumerate(pairs)]
    for copy in copies:
        copy.start()
    for copy in copies:
        copy.wait()
    slot = lax.broadcasted_iota(jnp.int32, (1, 128), 1)
    for a in range(2):
        for b in range(2):
            for z in range(2):
                for k in range(3):
                    own_ref[1 - a, 1 - b, z, k : k + 1, :] = off[k, a, b, z : z + 1, :]
                    own_ref[1 - a, 1 - b, z, 3 + k : 4 + k, :] = vel[k, a, b, z : z + 1, :]
                own_ref[1 - a, 1 - b, z, 6:7, :] = jnp.where(
                    slot < counts_ref[a, b, z], mass[a, b, z : z + 1, :], 0.0
                )
                own_ref[1 - a, 1 - b, z, 7:8, :] = energy[a, b, z : z + 1, :]


DENS_PAD = (1e3, 1e3, 1e3, 0, 0, 0, 0, 0)
DENS_ATTRS = (0, 1, 2, 6)
FORCE_PAD = (1e3, 1e3, 1e3, 0, 0, 0, 0, 0, 0, 0, 0.25, 0, 0, 0, 0, 0)
FORCE_ATTRS = (0, 1, 2, 3, 4, 5, 6, 8, 9, 10)


NEAR = [[(1, 0), (1, 1)], [(0, 0), (0, 1)]]
AHEAD = [[(1, 2), (1, 3)], [(0, 2), (0, 3)]]


def density_tiles(columns, own_ref, up_ref, right_ref, e_ref):
    for r, s in columns:
        for z in range(2):
            if r >= 2:
                tile = right_ref[r - 2, s, z]
            else:
                tile = up_ref[r, s - 2, z] if s >= 2 else own_ref[r, s, z]
            place(e_ref, cell_id(r, s, z), tile, r - 2, s - 2, z - 1)


def density_pack(groups, runs, e_ref, t_ref, j_ref):
    pad = pad_tile(DENS_PAD)
    starts, total = pack(groups, runs, lambda c: e_ref[c], t_ref, DENS_UNROLL, pad)
    spread(t_ref, j_ref, total, DENS_ATTRS, 8)
    return starts


def density_own(own_ref, sums_ref, j_ref, e_ref, t_ref):
    density_tiles(NEAR[0] + NEAR[1], own_ref, None, None, e_ref)
    starts = density_pack(cell_counts(e_ref, 0, 2), NEAR, e_ref, t_ref, j_ref)
    mine = [rows_of(e_ref, cell_id(1, 1, z), 3) for z in (0, 1)]
    sums = zeros(2)
    for row in starts:
        sums = density_loop(j_ref, row[0], row[2], mine, sums)
    for z in (0, 1):
        sums_ref[z] = sums[z]


def density_first(own_ref, up_ref, part_ref, jn_ref, sums_ref, j_ref, e_ref, t_ref):
    density_tiles(full(0) + full(1), own_ref, up_ref, None, e_ref)
    groups = cell_counts(e_ref, 0, 2)
    near, _ = lay(groups, NEAR, DENS_UNROLL)
    starts = density_pack(groups, AHEAD, e_ref, t_ref, j_ref)
    for b in (0, 1):
        mine = [rows_of(e_ref, cell_id(1, 1 + b, z), 3) for z in (0, 1)]
        sums = zeros(2) if b else tuple(part_ref[z] for z in (0, 1))
        for i in (0, 1):
            if b:
                sums = density_loop(jn_ref, near[i][1], near[i][2], mine, sums)
            sums = density_loop(j_ref, starts[i][0], starts[i][1 + b], mine, sums)
        for z in (0, 1):
            sums_ref[2 * b + z] = sums[z]


def density_last(
    own_ref, up_ref, right_ref, sums_ref, jn_ref, ja_ref, message_ref, e_ref, t_ref, j_ref
):
    density_tiles(full(1) + full(2) + full(3), own_ref, up_ref, right_ref, e_ref)
    groups = cell_counts(e_ref, 1, 4)
    near = lay(groups, NEAR[:1], DENS_UNROLL)[0][0]
    ahead = lay(groups, AHEAD[:1], DENS_UNROLL)[0][0]
    starts = density_pack(groups, [full(2), full(3)], e_ref, t_ref, j_ref)
    for a in (0, 1):
        for b in (0, 1):
            own = [cell_id(1 + a, 1 + b, z) for z in (0, 1)]
            mine = [rows_of(e_ref, o, 3) for o in own]
            if a == 0:
                sums = tuple(sums_ref[2 * b + z] for z in (0, 1))
            else:
                sums = zeros(2)
                sums = density_loop(jn_ref, near[b], near[2], mine, sums)
                sums = density_loop(ja_ref, ahead[0], ahead[1 + b], mine, sums)
            for i in (0,) if a == 0 else (0, 1):
                sums = density_loop(j_ref, starts[i][b], starts[i][b + 3], mine, sums)
            for z in (0, 1):
                rho = jnp.sum(sums[z], axis=0, keepdims=True) * SIGMA
                rho = jnp.where(e_ref[own[z], 6:7] > 0.0, rho, 1.0)
                n = 2 * (2 * a + b) + z
                message_ref[6, n : n + 1, :] = rho
    for z in (0, 1):
        message_ref[z] = own_ref[0, 1, z]
        message_ref[2 + z] = own_ref[1, 1, z]
        message_ref[4 + z] = right_ref[0, 1, z]


def force_tiles(columns, own_ref, up_ref, right_ref, sent_ref, down_ref, left_ref, e_ref, f_ref, c_ref):
    for r, s in columns:
        y = 2 - s
        c = cell_id(r, s, 0)
        for z in range(2):
            if r == 0:
                tile = left_ref[2 * (y + 1) + z]
            elif y == -1:
                tile = down_ref[2 * (r - 1) + z]
            elif r == 3:
                tile = right_ref[0, y, z]
            elif y == 2:
                tile = up_ref[r - 1, 0, z]
            else:
                tile = own_ref[r - 1, y, z]
            place(e_ref, c + z, tile, r - 2, y - 1, z - 1)
        n = 2 * (2 * (r % 2) + (y + 1) % 2)
        if r >= 2:
            source = sent_ref[6, n : n + 2] if y >= 1 else down_ref[6, n : n + 2]
        else:
            source = left_ref[8 if y >= 1 else 9, n : n + 2]
        f_ref[c : c + 2, :] = source
    low, high = 8 * columns[0][0], 8 * columns[-1][0] + 8
    energy = e_ref[low:high, 7, :]
    rho = f_ref[low:high]
    c_ref[0, low:high] = (2.0 / 3.0) * energy / rho
    c_ref[1, low:high] = 0.25 * jnp.sqrt((10.0 / 9.0) * energy)
    c_ref[2, low:high] = 0.25 * rho


def force_pack(groups, runs, e_ref, c_ref, t_ref, j_ref):
    def tile_of(c):
        rows = [e_ref[c]] + [c_ref[k, c : c + 1, :] for k in range(3)] + [jnp.zeros((5, 128), F)]
        return jnp.concatenate(rows, axis=0)

    starts, total = pack(groups, runs, tile_of, t_ref, FORCE_UNROLL, pad_tile(FORCE_PAD))
    spread(t_ref, j_ref, total, FORCE_ATTRS, 16)
    return starts


def force_rows(e_ref, c_ref, c):
    extra = [jnp.broadcast_to(c_ref[k, c : c + 1, :], (8, 128)) for k in range(3)]
    return rows_of(e_ref, c, 6) + extra


UPPER = [[(2, 0), (2, 1)], [(3, 0), (3, 1)]]
LOWER = [[(2, 2), (2, 3)], [(3, 2), (3, 3)]]


def force_upper(own_ref, up_ref, right_ref, sent_ref, sums_ref, j_ref, e_ref, f_ref, c_ref, t_ref):
    force_tiles(UPPER[0] + UPPER[1], own_ref, up_ref, right_ref, sent_ref, None, None, e_ref, f_ref, c_ref)
    starts = force_pack(cell_counts(e_ref, 2, 4), UPPER, e_ref, c_ref, t_ref, j_ref)
    mine = [force_rows(e_ref, c_ref, cell_id(2, 1, z)) for z in (0, 1)]
    sums = zeros(10)
    for row in starts:
        sums = force_loop(j_ref, row[0], row[2], mine, sums)
    for k in range(10):
        sums_ref[k] = sums[k]


def force_first(
    own_ref, up_ref, right_ref, sent_ref, down_ref, part_ref, ju_ref, sums_ref, j_ref,
    e_ref, f_ref, c_ref, t_ref,
):
    columns = full(2) + full(3)
    force_tiles(columns, own_ref, up_ref, right_ref, sent_ref, down_ref, None, e_ref, f_ref, c_ref)
    groups = cell_counts(e_ref, 2, 4)
    upper, _ = lay(groups, UPPER, FORCE_UNROLL)
    starts = force_pack(groups, LOWER, e_ref, c_ref, t_ref, j_ref)
    for b in (0, 1):
        mine = [force_rows(e_ref, c_ref, cell_id(2, 2 - b, z)) for z in (0, 1)]
        sums = tuple(part_ref[k] for k in range(10)) if b else zeros(10)
        for i in (0, 1):
            if not b:
                sums = force_loop(ju_ref, upper[i][1], upper[i][2], mine, sums)
            sums = force_loop(j_ref, starts[i][0], starts[i][2 - b], mine, sums)
        for k in range(10):
            sums_ref[10 * b + k] = sums[k]


def force_last(
    own_ref, up_ref, right_ref, sent_ref, down_ref, left_ref, sums_ref, ju_ref, jl_ref,
    dens_ref, acc_ref, heat_ref, e_ref, f_ref, c_ref, t_ref, j_ref,
):
    columns = full(0) + full(1) + full(2)
    force_tiles(columns, own_ref, up_ref, right_ref, sent_ref, down_ref, left_ref, e_ref, f_ref, c_ref)
    groups = cell_counts(e_ref, 0, 3)
    upper = lay(groups, UPPER[:1], FORCE_UNROLL)[0][0]
    lower = lay(groups, LOWER[:1], FORCE_UNROLL)[0][0]
    starts = force_pack(groups, [full(0), full(1)], e_ref, c_ref, t_ref, j_ref)
    for a in (0, 1):
        for b in (0, 1):
            own = [cell_id(1 + a, 2 - b, z) for z in (0, 1)]
            mine = [force_rows(e_ref, c_ref, o) for o in own]
            if a == 0:
                sums = zeros(10)
                sums = force_loop(ju_ref, upper[1 - b], upper[2], mine, sums)
                sums = force_loop(jl_ref, lower[0], lower[2 - b], mine, sums)
            else:
                sums = tuple(sums_ref[10 * b + k] for k in range(10))
            for r in (0, 1) if a == 0 else (1,):
                sums = force_loop(j_ref, starts[r][1 - b], starts[r][4 - b], mine, sums)
            for z in (0, 1):
                c = own[z]
                filled = jnp.where(e_ref[c, 6:7] > 0.0, 1.0, 0.0)
                scale = filled * (1.5 * SIGMA)
                s = [jnp.sum(sums[5 * z + k], axis=0, keepdims=True) * scale for k in range(5)]
                for k in range(3):
                    acc_ref[k, 1 - a, 1 - b, z : z + 1, :] = s[k]
                heat_ref[1 - a, 1 - b, z : z + 1, :] = -(c_ref[0, c : c + 1, :] * s[3] + 0.5 * s[4])
                dens_ref[1 - a, 1 - b, z : z + 1, :] = f_ref[c : c + 1, :] * filled


VMEM = pl.BlockSpec(memory_space=pltpu.VMEM)
HBM = pl.BlockSpec(memory_space=pltpu.HBM)
SMEM = pl.BlockSpec(memory_space=pltpu.SMEM)


def array(*shape):
    return jax.ShapeDtypeStruct(shape, F)


def call(kernel, name, outs, scratch, limit, flops, in_specs):
    return pl.pallas_call(
        kernel,
        name=name,
        out_shape=outs,
        in_specs=in_specs,
        out_specs=jax.tree.map(lambda _: VMEM, outs),
        scratch_shapes=scratch,
        cost_estimate=pl.CostEstimate(flops=flops, bytes_accessed=1 << 18, transcendentals=0),
        compiler_params=pltpu.CompilerParams(vmem_limit_bytes=limit * MIB),
    )


def shift(block, axis, step):
    count = lax.axis_size(axis)
    return lax.ppermute(block, axis, [((i + step) % count, i) for i in range(count)])


def shards(offsets, velocity, mass, energy, counts):
    tiles = pltpu.VMEM((32, 8, 128), F)
    packed = pltpu.VMEM((GROUPS, 8, 128), F)
    vector = pltpu.VMEM((3, 2, 2, 2, 128), F)
    scalar = pltpu.VMEM((2, 2, 2, 128), F)
    own = call(
        prepare_kernel, "prepare", array(2, 2, 2, 8, 128),
        [pltpu.SMEM((2, 2, 2), jnp.int32), vector, vector, scalar, scalar, pltpu.SemaphoreType.DMA((5,))],
        8, 1 << 16, [HBM] * 5,
    )(*[pltpu.with_memory_space_constraint(v, pltpu.HBM) for v in (counts, offsets, velocity, mass, energy)])
    half = pltpu.VMEM((HALF, 8, 128), F)
    up = shift(own, "gy", -1)
    part, near = call(
        density_own, "density_own", (array(2, 8, 128), array(4, HALF, 8, 128)),
        [tiles, half], 12, 1 << 26, [VMEM],
    )(own)
    part, up = lax.optimization_barrier((part, up))
    right = shift(jnp.concatenate([own, up], axis=1), "gx", -1)
    sums, ahead = call(
        density_first, "density_first", (array(4, 8, 128), array(4, HALF, 8, 128)),
        [tiles, half], 12, 1 << 27, [VMEM] * 4,
    )(own, up, part, near)
    sent = call(
        density_last, "density_last", array(7, 8, 128),
        [tiles, packed, pltpu.VMEM((4, GROUPS, 8, 128), F)], 16, 1 << 27, [VMEM] * 6,
    )(own, up, right, sums, near, ahead)
    down = shift(sent, "gy", 1)
    more = [tiles, pltpu.VMEM((32, 128), F), pltpu.VMEM((3, 32, 128), F)]
    part, upper = call(
        force_upper, "force_upper", (array(10, 8, 128), array(10, HALF, 8, 128)),
        more + [half], 16, 1 << 27, [VMEM] * 4,
    )(own, up, right, sent)
    part, down = lax.optimization_barrier((part, down))
    cols = [down[2:4], own[1].reshape(4, 8, 128), up[1, 0], sent[6:7], down[6:7]]
    left = shift(jnp.concatenate(cols, axis=0), "gx", 1)
    sums, lower = call(
        force_first, "force_first", (array(20, 8, 128), array(10, HALF, 8, 128)),
        more + [half], 16, 1 << 28, [VMEM] * 7,
    )(own, up, right, sent, down, part, upper)
    return call(
        force_last, "force_last", (array(2, 2, 2, 128), array(3, 2, 2, 2, 128), array(2, 2, 2, 128)),
        more + [packed, pltpu.VMEM((10, GROUPS, 8, 128), F)], 24, 1 << 28, [VMEM] * 9,
    )(own, up, right, sent, down, left, sums, upper, lower)


def solution(mesh):
    in_specs = (
        P(None, "gx", "gy", None, None),
        P(None, "gx", "gy", None, None),
        P("gx", "gy", None, None),
        P("gx", "gy", None, None),
        P("gx", "gy", None),
    )
    out_specs = (
        P("gx", "gy", None, None),
        P(None, "gx", "gy", None, None),
        P("gx", "gy", None, None),
    )
    return jax.shard_map(shards, mesh=mesh, in_specs=in_specs, out_specs=out_specs, check_vma=False)
```
